32 devices in a mesh: groups: 2 (over x), grid: 16 (over z, y, core).
Axes of the slice: x: 2, y: 2, z: 4, core: 2. Of those that a mesh axis runs over, the one named last changes fastest.
Arguments:
- spectra: bfloat16 [512, 4096], P('groups', 'grid'), parts along dimension 0, may hold values from -6 to 6
- response: bfloat16 [4096, 2048], P('grid'), may hold values from -0.09375 to 0.09375
- observed: float32 [1024, 32], P(('groups', 'grid')), parts along dimension 0, may hold values from -6 to 6
- inv_var: float32 [1024, 32], P(('groups', 'grid')), parts along dimension 0, may hold values from 0.5 to 4
- band_mask: int32 [1024, 32], P(('groups', 'grid')), parts along dimension 0, may hold values from 0 to 1
- det_counts: int32 [1024], P(('groups', 'grid')), parts along dimension 0, may hold values from 4 to 32
- anchor_bins: int32 [1024], P(('groups', 'grid')), parts along dimension 0, may hold values from -1 to 63, as said below
- init_weights: float32 [32768], P(('groups', 'grid')), parts along dimension 0, may hold values from 0.1 to 10
Outputs:
- weights: float32 [32768], P(('groups', 'grid')), parts along dimension 0
- posterior: float32 [64, 1024], P(None, ('groups', 'grid')), parts along dimension 1
The draws below stay inside these ranges and needn't reach their ends.
There are 2 independent parts, one for each index of `groups`. The reference program is written for one: setup_inputs(seed, part) draws one part's arguments, and reference() takes and returns one part's arrays. A program takes and returns all parts, laid end to end along the dimension named above; an argument that names none is the same for every part. Nothing has to cross between parts.
Inputs may be any that keep to these rules, and one draw needn't show every extreme that they name: `anchor_bins`: a bin index of 0 to 63 for a galaxy with a spectroscopic redshift, -1 for the others.
All inputs are finite; a program needn't handle non-finite values.
Results may differ from the reference program's by a relative error of at most 0.006.
The reference program's roundings to bfloat16 on the way count: a program that leaves them out, or rounds other values in their place, can miss the bound.
Values may be sent and summed in bfloat16 or wider, within the bound.
A program may use at most 64 MiB of HBM per device.

```python
import math
import jax
import jax.numpy as jnp
from jax import lax

WAVES = 4096
REDSHIFTS = 64
BANDS = 32
STEPS = 2
MODELS = 256
GALAXIES = 512


def bright_rows():
    return jnp.arange(GALAXIES, dtype=jnp.int32) % 64 == 0


def draw_observed(key, part):
    first = jax.random.fold_in(jax.random.fold_in(key, 11), 0)
    third = jax.random.fold_in(key, 12)
    values = jnp.clip(jax.random.normal(first, (GALAXIES, BANDS), jnp.float32), -6.0, 6.0)
    signs = 2.0 * jax.random.randint(third, (GALAXIES, BANDS), 0, 2).astype(jnp.float32) - 1.0
    values = jnp.where(bright_rows()[:, None], 6.0 * signs, values)
    return values.astype(jnp.float32)


def draw_inv_var(key, part):
    first = jax.random.fold_in(key, 31)
    values = jnp.exp(jax.random.uniform(first, (GALAXIES, BANDS), jnp.float32, math.log(0.5), math.log(4.0)))
    values = jnp.clip(values, 0.5, 4.0)
    values = jnp.where(bright_rows()[:, None], 4.0, values)
    return values.astype(jnp.float32)


def draw_band_mask(key, part):
    first = jax.random.fold_in(key, 37)
    values = (jax.random.randint(first, (GALAXIES, BANDS), 0, 8) < 7).astype(jnp.int32)
    values = jnp.where(bright_rows()[:, None], 1, values)
    return values.astype(jnp.int32)


def draw_det_counts(key, part):
    first = jax.random.fold_in(key, 41)
    values = jax.random.randint(first, (GALAXIES,), 4, BANDS + 1)
    values = jnp.where(bright_rows(), 4, values)
    return values.astype(jnp.int32)


def draw_anchor_bins(key, part):
    first, second = jax.random.split(jax.random.fold_in(key, 23))
    chosen = jax.random.randint(first, (GALAXIES,), 0, 4) == 0
    bins = jax.random.randint(second, (GALAXIES,), 0, REDSHIFTS)
    result = jnp.where(chosen, bins, -1).astype(jnp.int32)
    result = result.at[0].set(REDSHIFTS - 1)
    result = result.at[1].set(-1)
    return result


def levels(rng, dims, cuts, smallest, largest):
    loudness, own = 1.0, jax.random.fold_in(rng, 6)
    for dim, blocks in cuts:
        heights = jnp.exp(jax.random.uniform(jax.random.fold_in(own, dim), (blocks,), jnp.float32, smallest / len(cuts), largest / len(cuts)))
        loudness = loudness * jnp.repeat(heights, dims[dim] // blocks).reshape([-1 if axis == dim else 1 for axis in range(len(dims))])
    return loudness


def normal_values(stream_key, shape, spread, limit, cuts=(), held_as=jnp.bfloat16):
    factor_of = levels(stream_key, shape, cuts, -0.22, 0.18) if cuts else 1.0
    drawn = jax.random.normal(stream_key, shape, jnp.float32) * spread * factor_of
    return jnp.minimum(jnp.maximum(drawn, -limit), limit).astype(held_as)


def setup_inputs(seed: int = 0, part: int = 0) -> dict:
    key_of = jax.random.split(jax.random.key(seed), 9)
    part_keys = jax.random.split(jax.random.fold_in(key_of[8], part), 9)
    return {
        "spectra": normal_values(part_keys[0], (MODELS, WAVES), 1.0, 6.0, ((1, 16),)),
        "response": normal_values(key_of[1], (WAVES, REDSHIFTS * BANDS), WAVES ** -0.5, 0.09375, ((0, 16),)),
        "observed": draw_observed(jax.random.fold_in(jax.random.fold_in(key_of[8], part), 71), part),
        "inv_var": draw_inv_var(jax.random.fold_in(jax.random.fold_in(key_of[8], part), 71), part),
        "band_mask": draw_band_mask(jax.random.fold_in(jax.random.fold_in(key_of[8], part), 71), part),
        "det_counts": draw_det_counts(jax.random.fold_in(jax.random.fold_in(key_of[8], part), 71), part),
        "anchor_bins": draw_anchor_bins(jax.random.fold_in(jax.random.fold_in(key_of[8], part), 71), part),
        "init_weights": jnp.clip(jnp.exp(math.log(10.0) - 4.6051702 * jax.random.uniform(part_keys[7], (MODELS * REDSHIFTS,), jnp.float32) ** levels(part_keys[7], (MODELS * REDSHIFTS,), ((0, 16),), -0.2, 0.2)), 0.1, 10.0),
    }


excluded_score = -1.0e30


def model_columns(fluxes):
    shaped = fluxes.reshape(-1, REDSHIFTS, BANDS)
    joined = jnp.concatenate((-2.0 * shaped, shaped * shaped), axis=2)
    return joined.astype(jnp.bfloat16).reshape(-1, 2 * BANDS)


def galaxy_coeffs(observed, inv_var, band_mask, det_counts):
    masked_var = inv_var * band_mask.astype(jnp.float32)
    temper = 4.0 / (det_counts.astype(jnp.float32) + 8.0)
    joined = jnp.concatenate((masked_var * observed, masked_var), axis=1)
    return (temper[:, None] * joined).astype(jnp.bfloat16)


def block_scores(row_block, bin_block, model_cols):
    scores = -jnp.dot(row_block, model_cols.T, preferred_element_type=jnp.float32)
    column_bin = jnp.arange(model_cols.shape[0], dtype=jnp.int32) % REDSHIFTS
    allowed = (bin_block[:, None] < 0) | (bin_block[:, None] == column_bin[None, :])
    return jnp.where(allowed, scores, excluded_score)


def reference(spectra, response, observed, inv_var, band_mask, det_counts, anchor_bins, init_weights):
    fluxes = jnp.dot(spectra, response, preferred_element_type=jnp.float32)
    model_cols = model_columns(fluxes)
    coeffs = galaxy_coeffs(observed, inv_var, band_mask, det_counts)
    block = min(512, GALAXIES)
    count_blocks = GALAXIES // block
    row_blocks = coeffs.reshape(count_blocks, block, 2 * BANDS)
    bin_blocks = anchor_bins.reshape(count_blocks, block)
    weights = init_weights
    posterior = None
    for em_step in range(STEPS):
        def normalizer(pair, weights=weights):
            scores = block_scores(pair[0], pair[1], model_cols)
            peak = jnp.max(scores, axis=1)
            total = jnp.sum(weights[None, :] * jnp.exp(scores - peak[:, None]), axis=1)
            return peak + jnp.log(total)

        log_norm = lax.map(normalizer, (row_blocks, bin_blocks))

        def responsibilities(carry, triple, weights=weights):
            scores = block_scores(triple[0], triple[1], model_cols)
            shares = weights[None, :] * jnp.exp(scores - triple[2][:, None])
            return carry + jnp.sum(shares, axis=0), jnp.sum(shares.reshape(block, -1, REDSHIFTS), axis=1)

        mass, posterior = lax.scan(responsibilities, jnp.zeros((model_cols.shape[0],), jnp.float32), (row_blocks, bin_blocks, log_norm))
        weights = mass / GALAXIES
    return weights, posterior.reshape(GALAXIES, REDSHIFTS).T
```

```python
import functools

import jax
import jax.numpy as jnp
from jax import lax
from jax.experimental import pallas as pl
from jax.experimental.pallas import tpu as pltpu
from jax.sharding import PartitionSpec as P

REDSHIFTS = 64
BANDS = 32
STEPS = 2
LANES = 128
QUARTERS = LANES // BANDS
GROUPS_Z = REDSHIFTS // QUARTERS
CHUNKS = 4
MESH = pl.DeviceIdType.MESH
EXCLUDED = -1e30
HIGHEST = lax.Precision.HIGHEST


def iota(shape, dim):
    return lax.broadcasted_iota(jnp.int32, shape, dim)


def over_quarters(x, op):
    x = op(x, pltpu.roll(x, 64, 1))
    return op(x, pltpu.roll(x, 32, 1))


def body(
    n,
    galaxies,
    spectra_ref,
    response_ref,
    rows_ref,
    w_ref,
    outw_ref,
    outp_ref,
    part,
    got_a,
    got_b,
    got_c,
    all_rows,
    rt,
    penalty,
    cols,
    e_ref,
    wts,
    norms,
    x_ref,
    tots,
    post,
    got_post,
    a_send,
    a_recv,
    b_send,
    b_recv,
    c_send,
    c_recv,
    r_send,
    r_recv,
    n_send,
    n_recv,
    t_send,
    t_recv,
    p_send,
    p_recv,
):
    group = lax.axis_index("groups")
    me = lax.axis_index("grid")
    core = lax.rem(me, 2)
    yy = lax.rem(me // 2, 2)
    zz = me // 4
    nz = n // 4
    width = part.shape[-1]
    models = part.shape[-2]

    barrier = pltpu.get_barrier_semaphore()

    @pl.loop(1, n)
    def _(s):
        pl.semaphore_signal(
            barrier, inc=1, device_id=(group, lax.rem(me + s, n)), device_id_type=MESH
        )

    def flux_part(k):
        block = jnp.dot(
            spectra_ref[...],
            response_ref[:, k * width : (k + 1) * width],
            preferred_element_type=jnp.float32,
        )
        part[k] = block.reshape(nz, 2, 2, models, width)

    flux_part(0)
    pl.semaphore_wait(barrier, n - 1)

    def copy(src, dst, send, recv, target):
        return pltpu.make_async_remote_copy(
            src_ref=src,
            dst_ref=dst,
            send_sem=send,
            recv_sem=recv,
            device_id=(group, target),
            device_id_type=MESH,
        )

    def copy_a(k):
        return copy(
            part.at[k, :, :, 1 - core], got_a.at[k], a_send.at[k], a_recv.at[k], me + 1 - 2 * core
        )

    def copy_b(k):
        return copy(
            got_a.at[k, :, 1 - yy], got_b.at[k], b_send.at[k], b_recv.at[k], me + 2 - 4 * yy
        )

    def copy_c(k, s):
        to = lax.rem(zz + s, nz)
        return copy(
            got_b.at[k, to],
            got_c.at[k, s],
            c_send.at[k, s],
            c_recv.at[k, s],
            lax.rem(me + 4 * s, n),
        )

    copy_a(0).start()
    for k in range(1, CHUNKS):
        flux_part(k)
        copy_a(k).start()

    def spread(src, dst, send, recv, s):
        return copy(src, dst, send.at[s], recv.at[s], lax.rem(me + s, n))

    def rows_copy(s):
        return spread(rows_ref, all_rows.at[me], r_send, r_recv, s)

    all_rows[me] = rows_ref[...]

    for k in range(CHUNKS):
        copy_a(k).wait()
        for z in range(nz):
            for y in range(2):
                got_a[k, z, y] = got_a[k, z, y] + part[k, z, y, core]
        copy_b(k).start()

    @pl.loop(1, n)
    def _(s):
        rows_copy(s).start()

    for k in range(CHUNKS):
        copy_b(k).wait()
        for z in range(nz):
            got_b[k, z] = got_b[k, z] + got_a[k, z, yy]
        for s in range(1, nz):
            copy_c(k, s).start()

    eight = w_ref.shape[0]
    pick = (iota((models, eight), 0) // 2 == iota((models, eight), 1)).astype(jnp.float32)
    both = jnp.dot(pick, w_ref[...], precision=HIGHEST, preferred_element_type=jnp.float32)
    own = iota((models, LANES), 1) // REDSHIFTS == lax.rem(iota((models, LANES), 0), 2)
    both = jnp.where(own, both, 0.0)
    for j in range(GROUPS_Z):
        spot = lax.rem(iota((LANES, LANES), 0), REDSHIFTS) == 4 * j + iota((LANES, LANES), 1) // BANDS
        wts[j * models : (j + 1) * models, :] = jnp.dot(
            both, spot.astype(jnp.float32), precision=HIGHEST, preferred_element_type=jnp.float32
        )

    @pl.loop(1, n)
    def _(s):
        rows_copy(s).wait()

    lane = lax.rem(iota((LANES, 2 * LANES), 1), BANDS) + BANDS * (iota((LANES, 2 * LANES), 1) // LANES)
    tiles = (iota((LANES, 2 * LANES), 0) == lane).astype(jnp.bfloat16)
    keep = lax.rem(iota((LANES, 2 * LANES), 1), LANES) // BANDS == iota((LANES, 2 * LANES), 0) // BANDS
    anchor_row = (iota((GROUPS_Z, LANES), 1) == 2 * BANDS).astype(jnp.bfloat16)
    zbin = (QUARTERS * iota((GROUPS_Z, LANES), 0) + iota((GROUPS_Z, LANES), 1) // BANDS).astype(
        jnp.float32
    )

    @pl.loop(0, n)
    def _(d):
        x = all_rows[d]
        x = jnp.concatenate([x] * QUARTERS, axis=0)
        y = jnp.dot(x, tiles, preferred_element_type=jnp.float32)
        rt[d] = jnp.where(keep, y, 0.0).astype(jnp.bfloat16)
        anchors = lax.dot_general(
            anchor_row, x, (((1,), (1,)), ((), ())), preferred_element_type=jnp.float32
        )
        penalty[d] = jnp.where((anchors < 0) | (anchors == zbin), 0.0, EXCLUDED)

    per = width // LANES
    for k in range(CHUNKS):
        for s in range(1, nz):
            copy_c(k, s).wait()
        flux = got_b[k, zz]
        for s in range(1, nz):
            flux = flux + got_c[k, s]
        for i in range(per):
            j = k * per + i
            f = flux[:, i * LANES : (i + 1) * LANES]
            cols[j * models : (j + 1) * models, 0:LANES] = (2.0 * f).astype(jnp.bfloat16)
            cols[j * models : (j + 1) * models, LANES : 2 * LANES] = (-(f * f)).astype(jnp.bfloat16)

    rows_all = GROUPS_Z * models

    @pl.loop(0, n)
    def _(d):
        scores = lax.dot_general(
            cols[...], rt[d], (((1,), (1,)), ((), ())), preferred_element_type=jnp.float32
        )
        scores = scores.reshape(GROUPS_Z, models, LANES) + penalty[d][:, None, :]
        scores = scores.reshape(rows_all, LANES)
        peak = over_quarters(jnp.max(scores, axis=0, keepdims=True), jnp.maximum)
        e = jnp.exp(scores - peak)
        e_ref[d] = e
        total = over_quarters(jnp.sum(e * wts[...], axis=0, keepdims=True), jnp.add)
        norms[me, 0, pl.ds(d, 1), :] = peak
        norms[me, 1, pl.ds(d, 1), :] = total

    def norms_copy(s):
        return spread(norms.at[me], norms.at[me], n_send, n_recv, s)

    @pl.loop(1, n)
    def _(s):
        norms_copy(s).start()

    def norms_wait(s):
        src = lax.rem(me + n - s, n)
        return copy(norms.at[src], norms.at[src], n_send.at[s], n_recv.at[s], lax.rem(me + s, n))

    @pl.loop(1, n)
    def _(s):
        norms_wait(s).wait()

    top = norms[0, 0]
    for d in range(1, n):
        top = jnp.maximum(top, norms[d, 0])
    total = jnp.zeros_like(top)
    for d in range(n):
        total = total + norms[d, 1] * jnp.exp(norms[d, 0] - top)
    x_ref[0] = jnp.exp(norms[me, 0] - top)
    x_ref[1] = x_ref[0] / total

    same = (iota((LANES, LANES), 0) // BANDS == iota((LANES, LANES), 1) // BANDS).astype(jnp.float32)

    def new_weights():
        def add(d, acc):
            return acc + e_ref[d] * x_ref[1, pl.ds(d, 1), :]

        mass = lax.fori_loop(0, n, add, jnp.zeros((rows_all, LANES), jnp.float32))
        mass = jnp.dot(mass, same, precision=HIGHEST, preferred_element_type=jnp.float32)
        wts[...] = wts[...] * mass * (1.0 / galaxies)

    new_weights()

    @pl.loop(0, n)
    def _(d):
        v = (e_ref[d] * wts[...]).reshape(GROUPS_Z, models, LANES)
        u = jnp.sum(v, axis=1) * x_ref[0, pl.ds(d, 1), :]
        post[d] = u
        tots[me, pl.ds(d, 1), :] = over_quarters(jnp.sum(u, axis=0, keepdims=True), jnp.add)

    def tots_copy(s):
        return spread(tots.at[me], tots.at[me], t_send, t_recv, s)

    def post_copy(s):
        to = lax.rem(me + s, n)
        return copy(post.at[to], got_post.at[s], p_send.at[s], p_recv.at[s], to)

    @pl.loop(1, n)
    def _(s):
        tots_copy(s).start()

    @pl.loop(1, n)
    def _(s):
        post_copy(s).start()

    def tots_wait(s):
        src = lax.rem(me + n - s, n)
        return copy(tots.at[src], tots.at[src], t_send.at[s], t_recv.at[s], lax.rem(me + s, n))

    @pl.loop(1, n)
    def _(s):
        tots_wait(s).wait()

    total = tots[0]
    for d in range(1, n):
        total = total + tots[d]
    x_ref[1] = x_ref[0] / total
    new_weights()

    out = jnp.zeros((models, REDSHIFTS), jnp.float32)
    for j in range(GROUPS_Z):
        spot = iota((LANES, REDSHIFTS), 0) == BANDS * (iota((LANES, REDSHIFTS), 1) - 4 * j)
        out = out + jnp.dot(
            wts[j * models : (j + 1) * models, :],
            spot.astype(jnp.float32),
            precision=HIGHEST,
            preferred_element_type=jnp.float32,
        )
    outw_ref[...] = out

    @pl.loop(1, n)
    def _(s):
        post_copy(s).wait()

    mine = post[me]
    for s in range(1, n):
        mine = mine + got_post[s]
    whole = over_quarters(jnp.sum(mine, axis=0, keepdims=True), jnp.add)
    outp_ref[...] = mine / whole


def galaxy_rows(observed, inv_var, band_mask, det_counts, anchor_bins):
    masked_var = inv_var * band_mask.astype(jnp.float32)
    temper = 4.0 / (det_counts.astype(jnp.float32) + 8.0)
    joined = jnp.concatenate((masked_var * observed, masked_var), axis=1)
    joined = temper[:, None] * joined
    own = observed.shape[0]
    last = jnp.zeros((own, LANES - 2 * BANDS - 1), jnp.float32)
    anchors = anchor_bins.astype(jnp.float32)[:, None]
    return jnp.concatenate((joined, anchors, last), axis=1).astype(jnp.bfloat16)


def on_device(
    n, spectra, response, observed, inv_var, band_mask, det_counts, anchor_bins, init_weights
):
    rows = galaxy_rows(observed, inv_var, band_mask, det_counts, anchor_bins)
    own = observed.shape[0]
    models = spectra.shape[0] // n
    nz = n // 4
    width = response.shape[1] // CHUNKS
    f32, bf16 = jnp.float32, jnp.bfloat16
    dma = pltpu.SemaphoreType.DMA
    lanes_g = QUARTERS * own
    rows_all = GROUPS_Z * models
    weights, posterior = pl.pallas_call(
        functools.partial(body, n, own * n),
        out_shape=(
            jax.ShapeDtypeStruct((models, REDSHIFTS), f32),
            jax.ShapeDtypeStruct((GROUPS_Z, lanes_g), f32),
        ),
        in_specs=[pl.BlockSpec(memory_space=pltpu.VMEM)] * 4,
        out_specs=[pl.BlockSpec(memory_space=pltpu.VMEM)] * 2,
        scratch_shapes=[
            pltpu.VMEM((CHUNKS, nz, 2, 2, models, width), f32),
            pltpu.VMEM((CHUNKS, nz, 2, models, width), f32),
            pltpu.VMEM((CHUNKS, nz, models, width), f32),
            pltpu.VMEM((CHUNKS, nz, models, width), f32),
            pltpu.VMEM((n, own, LANES), bf16),
            pltpu.VMEM((n, LANES, 2 * LANES), bf16),
            pltpu.VMEM((n, GROUPS_Z, LANES), f32),
            pltpu.VMEM((rows_all, 2 * LANES), bf16),
            pltpu.VMEM((n, rows_all, LANES), f32),
            pltpu.VMEM((rows_all, LANES), f32),
            pltpu.VMEM((n, 2, n, LANES), f32),
            pltpu.VMEM((2, n, LANES), f32),
            pltpu.VMEM((n, n, LANES), f32),
            pltpu.VMEM((n, GROUPS_Z, LANES), f32),
            pltpu.VMEM((n, GROUPS_Z, LANES), f32),
            dma((CHUNKS,)),
            dma((CHUNKS,)),
            dma((CHUNKS,)),
            dma((CHUNKS,)),
            dma((CHUNKS, nz)),
            dma((CHUNKS, nz)),
        ]
        + [dma((n,))] * 8,
        compiler_params=pltpu.CompilerParams(
            collective_id=0, has_side_effects=True, vmem_limit_bytes=56 * 2**20
        ),
    )(spectra, response, rows, init_weights.reshape(-1, LANES))
    return weights.reshape(-1), posterior.reshape(REDSHIFTS, own)


def solution(mesh):
    return jax.shard_map(
        functools.partial(on_device, mesh.shape["grid"]),
        mesh=mesh,
        in_specs=(
            P("groups", "grid"),
            P("grid", None),
            P(("groups", "grid"), None),
            P(("groups", "grid"), None),
            P(("groups", "grid"), None),
            P(("groups", "grid")),
            P(("groups", "grid")),
            P(("groups", "grid")),
        ),
        out_specs=(P(("groups", "grid")), P(None, ("groups", "grid"))),
        check_vma=False,
    )
```

```python
import functools

import jax
import jax.numpy as jnp
from jax import lax
from jax.experimental import pallas as pl
from jax.experimental.pallas import tpu as pltpu
from jax.sharding import PartitionSpec as P

REDSHIFTS = 64
BANDS = 32
STEPS = 2
LANES = 128
QUARTERS = LANES // BANDS
GROUPS_Z = REDSHIFTS // QUARTERS
CHUNKS = 4
MESH = pl.DeviceIdType.MESH
EXCLUDED = -1e30
HIGHEST = lax.Precision.HIGHEST


def iota(shape, dim):
    return lax.broadcasted_iota(jnp.int32, shape, dim)


def over_quarters(x, op):
    x = op(x, pltpu.roll(x, 64, 1))
    return op(x, pltpu.roll(x, 32, 1))


def body(
    n,
    galaxies,
    spectra_ref,
    response_ref,
    obs_ref,
    ivar_ref,
    mask_ref,
    counts_ref,
    anchors_ref,
    w_ref,
    outw_ref,
    outp_ref,
    rows_f,
    part,
    got_a,
    got_b,
    got_c,
    all_rows,
    rt,
    penalty,
    cols,
    e_ref,
    wts,
    norms,
    x_ref,
    tots,
    post,
    got_post,
    a_send,
    a_recv,
    b_send,
    b_recv,
    c_send,
    c_recv,
    r_send,
    r_recv,
    n_send,
    n_recv,
    t_send,
    t_recv,
    p_send,
    p_recv,
):
    group = lax.axis_index("groups")
    me = lax.axis_index("grid")
    core = lax.rem(me, 2)
    yy = lax.rem(me // 2, 2)
    zz = me // 4
    nz = n // 4
    width = part.shape[-1]
    models = part.shape[-2]

    barrier = pltpu.get_barrier_semaphore()

    @pl.loop(1, n)
    def _(s):
        pl.semaphore_signal(
            barrier, inc=1, device_id=(group, lax.rem(me + s, n)), device_id_type=MESH
        )

    def flux_part(k):
        block = jnp.dot(
            spectra_ref[...],
            response_ref[:, k * width : (k + 1) * width],
            preferred_element_type=jnp.float32,
        )
        part[k] = block.reshape(nz, 2, 2, models, width)

    flux_part(0)

    own_g = obs_ref.shape[0]
    eye = iota((own_g, own_g), 0) == iota((own_g, own_g), 1)

    def column(row):
        return jnp.sum(jnp.where(eye, row, 0.0), axis=1, keepdims=True)

    masked_var = ivar_ref[...] * mask_ref[...].astype(jnp.float32)
    temper = column(4.0 / (counts_ref[...].astype(jnp.float32) + 8.0))
    rows_f[...] = jnp.broadcast_to(column(anchors_ref[...].astype(jnp.float32)), rows_f.shape)
    rows_f[:, 0:BANDS] = temper * (masked_var * obs_ref[...])
    rows_f[:, BANDS : 2 * BANDS] = temper * masked_var
    all_rows[me] = rows_f[...].astype(jnp.bfloat16)
    pl.semaphore_wait(barrier, n - 1)

    def copy(src, dst, send, recv, target):
        return pltpu.make_async_remote_copy(
            src_ref=src,
            dst_ref=dst,
            send_sem=send,
            recv_sem=recv,
            device_id=(group, target),
            device_id_type=MESH,
        )

    def copy_a(k):
        return copy(
            part.at[k, :, :, 1 - core], got_a.at[k], a_send.at[k], a_recv.at[k], me + 1 - 2 * core
        )

    def copy_b(k):
        return copy(
            got_a.at[k, :, 1 - yy], got_b.at[k], b_send.at[k], b_recv.at[k], me + 2 - 4 * yy
        )

    def copy_c(k, s):
        to = lax.rem(zz + s, nz)
        return copy(
            got_b.at[k, to],
            got_c.at[k, s],
            c_send.at[k, s],
            c_recv.at[k, s],
            lax.rem(me + 4 * s, n),
        )

    copy_a(0).start()
    for k in range(1, CHUNKS):
        flux_part(k)
        copy_a(k).start()

    def spread(src, dst, send, recv, s):
        return copy(src, dst, send.at[s], recv.at[s], lax.rem(me + s, n))

    def rows_copy(s):
        return spread(all_rows.at[me], all_rows.at[me], r_send, r_recv, s)


    for k in range(CHUNKS):
        copy_a(k).wait()
        for z in range(nz):
            for y in range(2):
                got_a[k, z, y] = got_a[k, z, y] + part[k, z, y, core]
        copy_b(k).start()

    @pl.loop(1, n)
    def _(s):
        rows_copy(s).start()

    for k in range(CHUNKS):
        copy_b(k).wait()
        for z in range(nz):
            got_b[k, z] = got_b[k, z] + got_a[k, z, yy]
        for s in range(1, nz):
            copy_c(k, s).start()

    eight = w_ref.shape[0]
    pick = (iota((models, eight), 0) // 2 == iota((models, eight), 1)).astype(jnp.float32)
    both = jnp.dot(pick, w_ref[...], precision=HIGHEST, preferred_element_type=jnp.float32)
    own = iota((models, LANES), 1) // REDSHIFTS == lax.rem(iota((models, LANES), 0), 2)
    both = jnp.where(own, both, 0.0)
    for j in range(GROUPS_Z):
        spot = lax.rem(iota((LANES, LANES), 0), REDSHIFTS) == 4 * j + iota((LANES, LANES), 1) // BANDS
        wts[j * models : (j + 1) * models, :] = jnp.dot(
            both, spot.astype(jnp.float32), precision=HIGHEST, preferred_element_type=jnp.float32
        )

    @pl.loop(1, n)
    def _(s):
        rows_copy(s).wait()

    lane = lax.rem(iota((LANES, 2 * LANES), 1), BANDS) + BANDS * (iota((LANES, 2 * LANES), 1) // LANES)
    tiles = (iota((LANES, 2 * LANES), 0) == lane).astype(jnp.bfloat16)
    keep = lax.rem(iota((LANES, 2 * LANES), 1), LANES) // BANDS == iota((LANES, 2 * LANES), 0) // BANDS
    anchor_row = (iota((GROUPS_Z, LANES), 1) == 2 * BANDS).astype(jnp.bfloat16)
    zbin = (QUARTERS * iota((GROUPS_Z, LANES), 0) + iota((GROUPS_Z, LANES), 1) // BANDS).astype(
        jnp.float32
    )

    @pl.loop(0, n, unroll=4)
    def _(d):
        x = all_rows[d]
        x = jnp.concatenate([x] * QUARTERS, axis=0)
        y = jnp.dot(x, tiles, preferred_element_type=jnp.float32)
        rt[d] = jnp.where(keep, y, 0.0).astype(jnp.bfloat16)
        anchors = lax.dot_general(
            anchor_row, x, (((1,), (1,)), ((), ())), preferred_element_type=jnp.float32
        )
        penalty[d] = jnp.where((anchors < 0) | (anchors == zbin), 0.0, EXCLUDED)

    per = width // LANES
    for k in range(CHUNKS):
        for s in range(1, nz):
            copy_c(k, s).wait()
        flux = got_b[k, zz]
        for s in range(1, nz):
            flux = flux + got_c[k, s]
        for i in range(per):
            j = k * per + i
            f = flux[:, i * LANES : (i + 1) * LANES]
            cols[j * models : (j + 1) * models, 0:LANES] = (2.0 * f).astype(jnp.bfloat16)
            cols[j * models : (j + 1) * models, LANES : 2 * LANES] = (-(f * f)).astype(jnp.bfloat16)

    rows_all = GROUPS_Z * models
    quarter = iota((1, LANES), 1) // BANDS
    norms[me] = jnp.zeros(norms.shape[1:], jnp.float32)
    tots[me] = jnp.zeros(tots.shape[1:], jnp.float32)

    def spread_out(slot, x):
        for q in range(QUARTERS):
            x_ref[slot, q] = over_quarters(jnp.where(quarter == q, x, 0.0), jnp.add)

    def factor(slot, d):
        return x_ref[slot, lax.rem(d, QUARTERS), pl.ds(d // QUARTERS, 1), :]

    @pl.loop(0, n, unroll=4)
    def _(d):
        scores = lax.dot_general(
            cols[...], rt[d], (((1,), (1,)), ((), ())), preferred_element_type=jnp.float32
        )
        scores = scores.reshape(GROUPS_Z, models, LANES) + penalty[d][:, None, :]
        scores = scores.reshape(rows_all, LANES)
        peak = over_quarters(jnp.max(scores, axis=0, keepdims=True), jnp.maximum)
        e = jnp.exp(scores - peak)
        e_ref[d] = e
        total = over_quarters(jnp.sum(e * wts[...], axis=0, keepdims=True), jnp.add)
        mine = quarter == lax.rem(d, QUARTERS)
        at = pl.ds(d // QUARTERS, 1)
        norms[me, 0, at, :] = jnp.where(mine, peak, norms[me, 0, at, :])
        norms[me, 1, at, :] = jnp.where(mine, total, norms[me, 1, at, :])

    def norms_copy(s):
        return spread(norms.at[me], norms.at[me], n_send, n_recv, s)

    @pl.loop(1, n)
    def _(s):
        norms_copy(s).start()

    def norms_wait(s):
        src = lax.rem(me + n - s, n)
        return copy(norms.at[src], norms.at[src], n_send.at[s], n_recv.at[s], lax.rem(me + s, n))

    @pl.loop(1, n)
    def _(s):
        norms_wait(s).wait()

    top = norms[0, 0]
    for d in range(1, n):
        top = jnp.maximum(top, norms[d, 0])
    total = jnp.zeros_like(top)
    for d in range(n):
        total = total + norms[d, 1] * jnp.exp(norms[d, 0] - top)
    shift = jnp.exp(norms[me, 0] - top)
    spread_out(1, shift / total)
    spread_out(0, shift)

    same = (iota((LANES, LANES), 0) // BANDS == iota((LANES, LANES), 1) // BANDS).astype(jnp.float32)

    def new_weights():
        def add(d, acc):
            return acc + e_ref[d] * factor(1, d)

        mass = lax.fori_loop(0, n, add, jnp.zeros((rows_all, LANES), jnp.float32), unroll=4)
        mass = jnp.dot(mass, same, precision=HIGHEST, preferred_element_type=jnp.float32)
        wts[...] = wts[...] * mass * (1.0 / galaxies)

    new_weights()

    @pl.loop(0, n, unroll=4)
    def _(d):
        v = (e_ref[d] * wts[...]).reshape(GROUPS_Z, models, LANES)
        u = jnp.sum(v, axis=1) * factor(0, d)
        post[d] = u
        total = over_quarters(jnp.sum(u, axis=0, keepdims=True), jnp.add)
        at = pl.ds(d // QUARTERS, 1)
        tots[me, at, :] = jnp.where(quarter == lax.rem(d, QUARTERS), total, tots[me, at, :])

    def tots_copy(s):
        return spread(tots.at[me], tots.at[me], t_send, t_recv, s)

    def post_copy(s):
        to = lax.rem(me + s, n)
        return copy(post.at[to], got_post.at[s], p_send.at[s], p_recv.at[s], to)

    @pl.loop(1, n)
    def _(s):
        tots_copy(s).start()

    @pl.loop(1, n)
    def _(s):
        post_copy(s).start()

    def tots_wait(s):
        src = lax.rem(me + n - s, n)
        return copy(tots.at[src], tots.at[src], t_send.at[s], t_recv.at[s], lax.rem(me + s, n))

    @pl.loop(1, n)
    def _(s):
        tots_wait(s).wait()

    total = tots[0]
    for d in range(1, n):
        total = total + tots[d]
    spread_out(1, shift / total)
    new_weights()

    out = jnp.zeros((models, REDSHIFTS), jnp.float32)
    for j in range(GROUPS_Z):
        spot = iota((LANES, REDSHIFTS), 0) == BANDS * (iota((LANES, REDSHIFTS), 1) - 4 * j)
        out = out + jnp.dot(
            wts[j * models : (j + 1) * models, :],
            spot.astype(jnp.float32),
            precision=HIGHEST,
            preferred_element_type=jnp.float32,
        )
    outw_ref[...] = out

    @pl.loop(1, n)
    def _(s):
        post_copy(s).wait()

    mine = post[me]
    for s in range(1, n):
        mine = mine + got_post[s]
    whole = over_quarters(jnp.sum(mine, axis=0, keepdims=True), jnp.add)
    mine = mine / whole
    for q in range(QUARTERS):
        outp_ref[pl.ds(q, GROUPS_Z, stride=QUARTERS), :] = mine[:, q * BANDS : (q + 1) * BANDS]


def on_device(
    n, spectra, response, observed, inv_var, band_mask, det_counts, anchor_bins, init_weights
):
    own = observed.shape[0]
    models = spectra.shape[0] // n
    nz = n // 4
    width = response.shape[1] // CHUNKS
    f32, bf16 = jnp.float32, jnp.bfloat16
    dma = pltpu.SemaphoreType.DMA
    rows_all = GROUPS_Z * models
    weights, posterior = pl.pallas_call(
        functools.partial(body, n, own * n),
        out_shape=(
            jax.ShapeDtypeStruct((models, REDSHIFTS), f32),
            jax.ShapeDtypeStruct((REDSHIFTS, own), f32),
        ),
        in_specs=[pl.BlockSpec(memory_space=pltpu.VMEM)] * 8,
        out_specs=[pl.BlockSpec(memory_space=pltpu.VMEM)] * 2,
        scratch_shapes=[
            pltpu.VMEM((own, LANES), f32),
            pltpu.VMEM((CHUNKS, nz, 2, 2, models, width), f32),
            pltpu.VMEM((CHUNKS, nz, 2, models, width), f32),
            pltpu.VMEM((CHUNKS, nz, models, width), f32),
            pltpu.VMEM((CHUNKS, nz, models, width), f32),
            pltpu.VMEM((n, own, LANES), bf16),
            pltpu.VMEM((n, LANES, 2 * LANES), bf16),
            pltpu.VMEM((n, GROUPS_Z, LANES), f32),
            pltpu.VMEM((rows_all, 2 * LANES), bf16),
            pltpu.VMEM((n, rows_all, LANES), f32),
            pltpu.VMEM((rows_all, LANES), f32),
            pltpu.VMEM((n, 2, nz, LANES), f32),
            pltpu.VMEM((2, QUARTERS, nz, LANES), f32),
            pltpu.VMEM((n, nz, LANES), f32),
            pltpu.VMEM((n, GROUPS_Z, LANES), f32),
            pltpu.VMEM((n, GROUPS_Z, LANES), f32),
            dma((CHUNKS,)),
            dma((CHUNKS,)),
            dma((CHUNKS,)),
            dma((CHUNKS,)),
            dma((CHUNKS, nz)),
            dma((CHUNKS, nz)),
        ]
        + [dma((n,))] * 8,
        compiler_params=pltpu.CompilerParams(
            collective_id=0, has_side_effects=True, vmem_limit_bytes=56 * 2**20
        ),
    )(
        spectra,
        response,
        observed,
        inv_var,
        band_mask,
        det_counts.reshape(1, own),
        anchor_bins.reshape(1, own),
        init_weights.reshape(-1, LANES),
    )
    return weights.reshape(-1), posterior


def solution(mesh):
    return jax.shard_map(
        functools.partial(on_device, mesh.shape["grid"]),
        mesh=mesh,
        in_specs=(
            P("groups", "grid"),
            P("grid", None),
            P(("groups", "grid"), None),
            P(("groups", "grid"), None),
            P(("groups", "grid"), None),
            P(("groups", "grid")),
            P(("groups", "grid")),
            P(("groups", "grid")),
        ),
        out_specs=(P(("groups", "grid")), P(None, ("groups", "grid"))),
        check_vma=False,
    )
```

```python
import functools

import jax
import jax.numpy as jnp
from jax import lax
from jax.experimental import pallas as pl
from jax.experimental.pallas import tpu as pltpu
from jax.sharding import PartitionSpec as P

REDSHIFTS = 64
BANDS = 32
STEPS = 2
LANES = 128
QUARTERS = LANES // BANDS
GROUPS_Z = REDSHIFTS // QUARTERS
CHUNKS = 4
MESH = pl.DeviceIdType.MESH
EXCLUDED = -1e30
HIGHEST = lax.Precision.HIGHEST


def iota(shape, dim):
    return lax.broadcasted_iota(jnp.int32, shape, dim)


def over_quarters(x, op):
    x = op(x, pltpu.roll(x, 64, 1))
    return op(x, pltpu.roll(x, 32, 1))


def body(
    n,
    galaxies,
    spectra_ref,
    response_ref,
    obs_ref,
    ivar_ref,
    mask_ref,
    counts_ref,
    anchors_ref,
    w_ref,
    outw_ref,
    outp_ref,
    rows_f,
    part,
    got_a,
    got_b,
    got_c,
    all_rows,
    rt,
    penalty,
    cols,
    e_ref,
    wts,
    norms,
    x_ref,
    tots,
    post,
    got_post,
    a_send,
    a_recv,
    b_send,
    b_recv,
    c_send,
    c_recv,
    r_send,
    r_recv,
    n_send,
    n_recv,
    t_send,
    t_recv,
    p_send,
    p_recv,
):
    group = lax.axis_index("groups")
    me = lax.axis_index("grid")
    core = lax.rem(me, 2)
    yy = lax.rem(me // 2, 2)
    zz = me // 4
    nz = n // 4
    width = part.shape[-1]
    models = part.shape[-2]

    barrier = pltpu.get_barrier_semaphore()

    @pl.loop(1, n)
    def _(s):
        pl.semaphore_signal(
            barrier, inc=1, device_id=(group, lax.rem(me + s, n)), device_id_type=MESH
        )

    def flux_part(k):
        block = jnp.dot(
            spectra_ref[...],
            response_ref[:, k * width : (k + 1) * width],
            preferred_element_type=jnp.float32,
        )
        part[k] = block.reshape(nz, 2, 2, models, width)

    flux_part(0)

    own_g = obs_ref.shape[0]
    eye = iota((own_g, own_g), 0) == iota((own_g, own_g), 1)

    def column(row):
        return jnp.sum(jnp.where(eye, row, 0.0), axis=1, keepdims=True)

    masked_var = ivar_ref[...] * mask_ref[...].astype(jnp.float32)
    temper = column(4.0 / (counts_ref[...].astype(jnp.float32) + 8.0))
    rows_f[...] = jnp.broadcast_to(column(anchors_ref[...].astype(jnp.float32)), rows_f.shape)
    rows_f[:, 0:BANDS] = temper * (masked_var * obs_ref[...])
    rows_f[:, BANDS : 2 * BANDS] = temper * masked_var
    all_rows[me] = rows_f[...].astype(jnp.bfloat16)
    pl.semaphore_wait(barrier, n - 1)

    def copy(src, dst, send, recv, target):
        return pltpu.make_async_remote_copy(
            src_ref=src,
            dst_ref=dst,
            send_sem=send,
            recv_sem=recv,
            device_id=(group, target),
            device_id_type=MESH,
        )

    def copy_a(k):
        return copy(
            part.at[k, :, :, 1 - core], got_a.at[k], a_send.at[k], a_recv.at[k], me + 1 - 2 * core
        )

    def copy_b(k):
        return copy(
            got_a.at[k, :, 1 - yy], got_b.at[k], b_send.at[k], b_recv.at[k], me + 2 - 4 * yy
        )

    def copy_c(k, s):
        to = lax.rem(zz + s, nz)
        return copy(
            got_b.at[k, to],
            got_c.at[k, s],
            c_send.at[k, s],
            c_recv.at[k, s],
            lax.rem(me + 4 * s, n),
        )

    copy_a(0).start()
    for k in range(1, CHUNKS):
        flux_part(k)
        copy_a(k).start()

    def spread(src, dst, send, recv, s):
        return copy(src, dst, send.at[s], recv.at[s], lax.rem(me + s, n))

    def rows_copy(s):
        return spread(all_rows.at[me], all_rows.at[me], r_send, r_recv, s)


    for k in range(CHUNKS):
        copy_a(k).wait()
        for z in range(nz):
            for y in range(2):
                got_a[k, z, y] = got_a[k, z, y] + part[k, z, y, core]
        copy_b(k).start()

    @pl.loop(1, n)
    def _(s):
        rows_copy(s).start()

    for k in range(CHUNKS):
        copy_b(k).wait()
        for z in range(nz):
            got_b[k, z] = got_b[k, z] + got_a[k, z, yy]
        for s in range(1, nz):
            copy_c(k, s).start()

    eight = w_ref.shape[0]
    pick = (iota((models, eight), 0) // 2 == iota((models, eight), 1)).astype(jnp.float32)
    both = jnp.dot(pick, w_ref[...], precision=HIGHEST, preferred_element_type=jnp.float32)
    own = iota((models, LANES), 1) // REDSHIFTS == lax.rem(iota((models, LANES), 0), 2)
    both = jnp.where(own, both, 0.0)
    for j in range(GROUPS_Z):
        spot = lax.rem(iota((LANES, LANES), 0), REDSHIFTS) == 4 * j + iota((LANES, LANES), 1) // BANDS
        wts[j * models : (j + 1) * models, :] = jnp.dot(
            both, spot.astype(jnp.float32), precision=HIGHEST, preferred_element_type=jnp.float32
        )

    @pl.loop(1, n)
    def _(s):
        rows_copy(s).wait()

    lane = lax.rem(iota((LANES, 2 * LANES), 1), BANDS) + BANDS * (iota((LANES, 2 * LANES), 1) // LANES)
    tiles = (iota((LANES, 2 * LANES), 0) == lane).astype(jnp.bfloat16)
    keep = lax.rem(iota((LANES, 2 * LANES), 1), LANES) // BANDS == iota((LANES, 2 * LANES), 0) // BANDS
    anchor_row = (iota((GROUPS_Z, LANES), 1) == 2 * BANDS).astype(jnp.bfloat16)
    zbin = (QUARTERS * iota((GROUPS_Z, LANES), 0) + iota((GROUPS_Z, LANES), 1) // BANDS).astype(
        jnp.float32
    )

    @pl.loop(0, n, unroll=8)
    def _(d):
        x = all_rows[d]
        x = jnp.concatenate([x] * QUARTERS, axis=0)
        y = jnp.dot(x, tiles, preferred_element_type=jnp.float32)
        rt[d] = jnp.where(keep, y, 0.0).astype(jnp.bfloat16)
        anchors = lax.dot_general(
            anchor_row, x, (((1,), (1,)), ((), ())), preferred_element_type=jnp.float32
        )
        penalty[d] = jnp.where((anchors < 0) | (anchors == zbin), 0.0, EXCLUDED)

    per = width // LANES
    for k in range(CHUNKS):
        for s in range(1, nz):
            copy_c(k, s).wait()
        flux = got_b[k, zz]
        for s in range(1, nz):
            flux = flux + got_c[k, s]
        for i in range(per):
            j = k * per + i
            f = flux[:, i * LANES : (i + 1) * LANES]
            cols[j * models : (j + 1) * models, 0:LANES] = (2.0 * f).astype(jnp.bfloat16)
            cols[j * models : (j + 1) * models, LANES : 2 * LANES] = (-(f * f)).astype(jnp.bfloat16)

    rows_all = GROUPS_Z * models
    quarter = iota((1, LANES), 1) // BANDS
    norms[me] = jnp.zeros(norms.shape[1:], jnp.float32)
    tots[me] = jnp.zeros(tots.shape[1:], jnp.float32)

    def spread_out(slot, x):
        for q in range(QUARTERS):
            x_ref[slot, q] = over_quarters(jnp.where(quarter == q, x, 0.0), jnp.add)

    def factor(slot, d):
        return x_ref[slot, lax.rem(d, QUARTERS), pl.ds(d // QUARTERS, 1), :]

    @pl.loop(0, n, unroll=8)
    def _(d):
        scores = lax.dot_general(
            cols[...], rt[d], (((1,), (1,)), ((), ())), preferred_element_type=jnp.float32
        )
        scores = scores.reshape(GROUPS_Z, models, LANES) + penalty[d][:, None, :]
        scores = scores.reshape(rows_all, LANES)
        peak = over_quarters(jnp.max(scores, axis=0, keepdims=True), jnp.maximum)
        e = jnp.exp(scores - peak)
        e_ref[d] = e
        total = over_quarters(jnp.sum(e * wts[...], axis=0, keepdims=True), jnp.add)
        mine = quarter == lax.rem(d, QUARTERS)
        at = pl.ds(d // QUARTERS, 1)
        norms[me, 0, at, :] = jnp.where(mine, peak, norms[me, 0, at, :])
        norms[me, 1, at, :] = jnp.where(mine, total, norms[me, 1, at, :])

    def norms_copy(s):
        return spread(norms.at[me], norms.at[me], n_send, n_recv, s)

    @pl.loop(1, n)
    def _(s):
        norms_copy(s).start()

    def norms_wait(s):
        src = lax.rem(me + n - s, n)
        return copy(norms.at[src], norms.at[src], n_send.at[s], n_recv.at[s], lax.rem(me + s, n))

    @pl.loop(1, n)
    def _(s):
        norms_wait(s).wait()

    top = norms[0, 0]
    for d in range(1, n):
        top = jnp.maximum(top, norms[d, 0])
    total = jnp.zeros_like(top)
    for d in range(n):
        total = total + norms[d, 1] * jnp.exp(norms[d, 0] - top)
    shift = jnp.exp(norms[me, 0] - top)
    spread_out(1, shift / total)
    spread_out(0, shift)

    same = (iota((LANES, LANES), 0) // BANDS == iota((LANES, LANES), 1) // BANDS).astype(jnp.float32)

    def new_weights():
        def add(d, acc):
            return acc + e_ref[d] * factor(1, d)

        mass = lax.fori_loop(0, n, add, jnp.zeros((rows_all, LANES), jnp.float32), unroll=8)
        mass = jnp.dot(mass, same, precision=HIGHEST, preferred_element_type=jnp.float32)
        wts[...] = wts[...] * mass * (1.0 / galaxies)

    new_weights()

    @pl.loop(0, n, unroll=8)
    def _(d):
        v = (e_ref[d] * wts[...]).reshape(GROUPS_Z, models, LANES)
        u = jnp.sum(v, axis=1) * factor(0, d)
        post[d] = u
        total = over_quarters(jnp.sum(u, axis=0, keepdims=True), jnp.add)
        at = pl.ds(d // QUARTERS, 1)
        tots[me, at, :] = jnp.where(quarter == lax.rem(d, QUARTERS), total, tots[me, at, :])

    def tots_copy(s):
        return spread(tots.at[me], tots.at[me], t_send, t_recv, s)

    def post_copy(s):
        to = lax.rem(me + s, n)
        return copy(post.at[to], got_post.at[s], p_send.at[s], p_recv.at[s], to)

    @pl.loop(1, n)
    def _(s):
        tots_copy(s).start()

    @pl.loop(1, n)
    def _(s):
        post_copy(s).start()

    def tots_wait(s):
        src = lax.rem(me + n - s, n)
        return copy(tots.at[src], tots.at[src], t_send.at[s], t_recv.at[s], lax.rem(me + s, n))

    @pl.loop(1, n)
    def _(s):
        tots_wait(s).wait()

    total = tots[0]
    for d in range(1, n):
        total = total + tots[d]
    spread_out(1, shift / total)
    new_weights()

    out = jnp.zeros((models, REDSHIFTS), jnp.float32)
    for j in range(GROUPS_Z):
        spot = iota((LANES, REDSHIFTS), 0) == BANDS * (iota((LANES, REDSHIFTS), 1) - 4 * j)
        out = out + jnp.dot(
            wts[j * models : (j + 1) * models, :],
            spot.astype(jnp.float32),
            precision=HIGHEST,
            preferred_element_type=jnp.float32,
        )
    rows_f[0:models, 0:REDSHIFTS] = out
    for h in range(2):
        outw_ref[:, h * REDSHIFTS : (h + 1) * REDSHIFTS] = rows_f[
            pl.ds(h, models // 2, stride=2), 0:REDSHIFTS
        ]

    @pl.loop(1, n)
    def _(s):
        post_copy(s).wait()

    mine = post[me]
    for s in range(1, n):
        mine = mine + got_post[s]
    whole = over_quarters(jnp.sum(mine, axis=0, keepdims=True), jnp.add)
    mine = mine / whole
    for q in range(QUARTERS):
        outp_ref[pl.ds(q, GROUPS_Z, stride=QUARTERS), :] = mine[:, q * BANDS : (q + 1) * BANDS]


def on_device(
    n, spectra, response, observed, inv_var, band_mask, det_counts, anchor_bins, init_weights
):
    own = observed.shape[0]
    models = spectra.shape[0] // n
    nz = n // 4
    width = response.shape[1] // CHUNKS
    f32, bf16 = jnp.float32, jnp.bfloat16
    dma = pltpu.SemaphoreType.DMA
    rows_all = GROUPS_Z * models
    weights, posterior = pl.pallas_call(
        functools.partial(body, n, own * n),
        out_shape=(
            jax.ShapeDtypeStruct((models // 2, LANES), f32),
            jax.ShapeDtypeStruct((REDSHIFTS, own), f32),
        ),
        in_specs=[pl.BlockSpec(memory_space=pltpu.VMEM)] * 8,
        out_specs=[pl.BlockSpec(memory_space=pltpu.VMEM)] * 2,
        scratch_shapes=[
            pltpu.VMEM((own, LANES), f32),
            pltpu.VMEM((CHUNKS, nz, 2, 2, models, width), f32),
            pltpu.VMEM((CHUNKS, nz, 2, models, width), f32),
            pltpu.VMEM((CHUNKS, nz, models, width), f32),
            pltpu.VMEM((CHUNKS, nz, models, width), f32),
            pltpu.VMEM((n, own, LANES), bf16),
            pltpu.VMEM((n, LANES, 2 * LANES), bf16),
            pltpu.VMEM((n, GROUPS_Z, LANES), f32),
            pltpu.VMEM((rows_all, 2 * LANES), bf16),
            pltpu.VMEM((n, rows_all, LANES), f32),
            pltpu.VMEM((rows_all, LANES), f32),
            pltpu.VMEM((n, 2, nz, LANES), f32),
            pltpu.VMEM((2, QUARTERS, nz, LANES), f32),
            pltpu.VMEM((n, nz, LANES), f32),
            pltpu.VMEM((n, GROUPS_Z, LANES), f32),
            pltpu.VMEM((n, GROUPS_Z, LANES), f32),
            dma((CHUNKS,)),
            dma((CHUNKS,)),
            dma((CHUNKS,)),
            dma((CHUNKS,)),
            dma((CHUNKS, nz)),
            dma((CHUNKS, nz)),
        ]
        + [dma((n,))] * 8,
        compiler_params=pltpu.CompilerParams(
            collective_id=0, has_side_effects=True, vmem_limit_bytes=56 * 2**20
        ),
    )(
        spectra,
        response,
        observed,
        inv_var,
        band_mask,
        det_counts.reshape(1, own),
        anchor_bins.reshape(1, own),
        init_weights.reshape(-1, LANES),
    )
    return weights.reshape(-1), posterior


def solution(mesh):
    return jax.shard_map(
        functools.partial(on_device, mesh.shape["grid"]),
        mesh=mesh,
        in_specs=(
            P("groups", "grid"),
            P("grid", None),
            P(("groups", "grid"), None),
            P(("groups", "grid"), None),
            P(("groups", "grid"), None),
            P(("groups", "grid")),
            P(("groups", "grid")),
            P(("groups", "grid")),
        ),
        out_specs=(P(("groups", "grid")), P(None, ("groups", "grid"))),
        check_vma=False,
    )
```
